32 devices in a mesh: space: 16 (over z, y, x), mem: 2 (over core).
Axes of the slice: x: 2, y: 2, z: 4, core: 2. Of those that a mesh axis runs over, the one named last changes fastest.
Arguments:
- perturb: float32 [1024, 4096], P(('space', 'mem')), may hold values from -6 to 6
- pair_list: int32 [64, 3], P('space'), may hold values from 0 to 15, as said below
- pair_count: int32 [16], P('space'), may hold values from 1 to 4, as said below
- band_weight: float32 [8], replicated, may hold values from 0.25 to 1
- cov_scale: float32 [1], replicated, may hold values from 0.5 to 2
- target: float32 [4096, 1024], P('space', 'mem'), may hold values from -6 to 6
- first_guess: float32 [4096, 1024], P('space', 'mem'), may hold values from -6 to 6
Outputs:
- solution: float32 [4096, 1024], P('space', 'mem')
The draws below stay inside these ranges and needn't reach their ends.
Inputs may be any that keep to these rules, and one draw needn't show every extreme that they name: `pair_list`: rows 4 * s to 4 * s + 3 are owner s's slots. The first block of each is owner s's own block s; the second is the first plus d modulo 16, with 0 <= d <= 3; each of the four pairs (d = 0 to 3) stands in exactly one slot of its owner. The third column is an index into band_weight. Only the first pair_count[s] slots of owner s are live; in every draw some owner has all 4 slots live.
All inputs are finite; a program needn't handle non-finite values.
Results may differ from the reference program's by a relative error of at most 0.0003.
Values sent between devices are 32-bit elements; how exact they have to be, the bound alone decides.
A program may use at most 64 MiB of HBM per device.

```python
import math
import jax
import jax.numpy as jnp
from jax import lax

BLOCK = 256
MEMBERS = 1024
COLS = 1024
BLK_DEV = 1
REACH_DEV = 3
NBANDS = 8
ITERS = 2
CAP = 4
ROWS = 4096
NBLK = 16
PAIRS = 64


def pair_tables(key):
    owners = PAIRS // CAP
    reach = REACH_DEV * BLK_DEV
    subkeys = jax.random.split(jax.random.fold_in(key, 11), owners)
    orders = jax.vmap(lambda subkey: jax.random.permutation(subkey, CAP))(subkeys).astype(jnp.int32)
    starts = (jnp.arange(owners, dtype=jnp.int32) * BLK_DEV)[:, None]
    first_block = starts + orders // (reach + 1)
    gap = orders % (reach + 1)
    second_block = (first_block + gap) % NBLK
    jitter = jax.random.randint(jax.random.fold_in(key, 12), (owners, CAP), 0, 2)
    band = jnp.minimum(NBANDS - 1, gap * 4 // reach + jitter)
    pairs = jnp.stack([first_block, second_block, band], -1).reshape(PAIRS, 3).astype(jnp.int32)
    lower = jax.random.randint(jax.random.fold_in(key, 13), (owners,), 1, CAP + 1)
    upper = jax.random.randint(jax.random.fold_in(key, 14), (owners,), 1, CAP + 1)
    counts = jnp.minimum(lower, upper)
    hottest = jax.random.randint(jax.random.fold_in(key, 15), (), 0, owners)
    counts = counts.at[hottest].set(CAP).astype(jnp.int32)
    return (pairs, counts)


def draw_pair_list(key, part):
    return pair_tables(jax.random.fold_in(key, 7))[0]


def draw_pair_count(key, part):
    return pair_tables(jax.random.fold_in(key, 7))[1]


def level_of(rng, shape, cuts, least, top_value):
    def one(position, blocks):
        heights = jax.random.uniform(jax.random.fold_in(jax.random.fold_in(rng, 6), position), (blocks,), jnp.float32, least / len(cuts), top_value / len(cuts))
        return jnp.repeat(jnp.exp(heights), shape[position] // blocks).reshape((-1,) + (1,) * (len(shape) - position - 1))

    factor_of = one(*cuts[0])
    for cut in cuts[1:]:
        factor_of = factor_of * one(*cut)
    return factor_of


def bell_draw(own_key, extent, spread, limit, cuts=(), kind=jnp.bfloat16):
    array = spread * jax.random.normal(own_key, extent, jnp.float32)
    if cuts:
        array = array * level_of(own_key, extent, cuts, -0.22, 0.18)
    return jnp.clip(array, -limit, limit).astype(kind)


def setup_inputs(seed: int = 0) -> dict:
    splits = jax.random.split(jax.random.key(seed), 8)
    perturb = bell_draw(splits[0], (MEMBERS, ROWS), 1.0, 6.0, ((0, 32),), jnp.float32)
    pair_list = draw_pair_list(jax.random.fold_in(splits[7], 71), 0)
    pair_count = draw_pair_count(jax.random.fold_in(splits[7], 71), 0)
    band_weight = jnp.clip(jnp.exp(jax.random.uniform(splits[3], (NBANDS,), jnp.float32, math.log(0.25), math.log(1.0))), 0.25, 1.0)
    cov_scale = jnp.clip(jax.random.uniform(splits[4], (1,), jnp.float32, 0.5, 2.0), 0.5, 2.0)
    target = bell_draw(splits[5], (ROWS, COLS), 1.0, 6.0, ((0, 16), (1, 2)), jnp.float32)
    first_guess = bell_draw(splits[6], (ROWS, COLS), 1.0, 6.0, ((0, 16), (1, 2)), jnp.float32)
    return dict(perturb=perturb, pair_list=pair_list, pair_count=pair_count, band_weight=band_weight, cov_scale=cov_scale, target=target, first_guess=first_guess)


def reference(perturb, pair_list, pair_count, band_weight, cov_scale, target, first_guess):
    numbers = jnp.arange(PAIRS, dtype=jnp.int32)
    owners = numbers // CAP
    slot_ids = numbers % CAP
    living = (slot_ids < pair_count[owners]).astype(jnp.float32)
    weights = cov_scale[0] * band_weight[pair_list[:, 2]] * living / (MEMBERS - 1)

    def build_tile(number):
        first_cols = lax.dynamic_slice_in_dim(perturb, (pair_list[number, 0] * BLOCK).astype(jnp.int32), BLOCK, 1)
        second_cols = lax.dynamic_slice_in_dim(perturb, (pair_list[number, 1] * BLOCK).astype(jnp.int32), BLOCK, 1)
        return jnp.dot(first_cols.T, second_cols, precision=lax.Precision.HIGHEST, preferred_element_type=jnp.float32) * weights[number]

    tiles = lax.map(build_tile, numbers)

    def apply_cov(iterate):
        def advance(running, number):
            first_row = (pair_list[number, 0] * BLOCK).astype(jnp.int32)
            second_row = (pair_list[number, 1] * BLOCK).astype(jnp.int32)
            tile_now = tiles[number]
            own_rows = lax.dynamic_slice_in_dim(iterate, first_row, BLOCK, 0)
            near_rows = lax.dynamic_slice_in_dim(iterate, second_row, BLOCK, 0)
            forward = jnp.dot(tile_now, near_rows, precision=lax.Precision.HIGHEST, preferred_element_type=jnp.float32)
            mirror = jnp.dot(tile_now.T, own_rows, precision=lax.Precision.HIGHEST, preferred_element_type=jnp.float32)
            mirror = mirror * (pair_list[number, 0] != pair_list[number, 1]).astype(jnp.float32)
            running = lax.dynamic_update_slice_in_dim(running, lax.dynamic_slice_in_dim(running, first_row, BLOCK, 0) + forward, first_row, 0)
            running = lax.dynamic_update_slice_in_dim(running, lax.dynamic_slice_in_dim(running, second_row, BLOCK, 0) + mirror, second_row, 0)
            return running, None

        total, unused = lax.scan(advance, jnp.zeros_like(iterate), numbers)
        return total

    iterate = first_guess
    for sweep in range(ITERS):
        iterate = iterate + 0.5 * (target - iterate - apply_cov(iterate))
    return iterate
```

```python
import jax
import jax.numpy as jnp
from jax import lax
from jax.sharding import PartitionSpec as P

BLOCK = 256
MEMBERS = 1024
REACH_DEV = 3
NBANDS = 8
ITERS = 2


def shifted(array, axis, by):
    count = lax.axis_size(axis)
    return lax.ppermute(array, axis, [(i, (i + by) % count) for i in range(count)])


def mm(a, b, ca, cb):
    return lax.dot_general(
        a, b, (((ca,), (cb,)), ((), ())), precision=lax.Precision.HIGH,
        preferred_element_type=jnp.float32,
    )


def gap_weights(pair_list, pair_count, band_weight, cov_scale):
    slots = pair_list.shape[0]
    blocks_all = lax.axis_size("space")
    gap = (pair_list[:, 1] - pair_list[:, 0]) % blocks_all
    living = (jnp.arange(slots, dtype=jnp.int32) < pair_count[0]).astype(jnp.float32)
    bands = jnp.arange(NBANDS, dtype=jnp.int32)
    band_now = jnp.sum(
        jnp.where(pair_list[:, 2][:, None] == bands[None, :], band_weight[None, :], 0.0), axis=1
    )
    slot_weight = cov_scale[0] * band_now * living / (MEMBERS - 1)
    gaps = jnp.arange(REACH_DEV + 1, dtype=jnp.int32)
    return jnp.sum(jnp.where(gap[:, None] == gaps[None, :], slot_weight[:, None], 0.0), axis=0)


def per_device(perturb, pair_list, pair_count, band_weight, cov_scale, target, first_guess):
    w = gap_weights(pair_list, pair_count, band_weight, cov_scale)
    w_next = shifted(w, "space", -1)
    p0 = lax.all_to_all(perturb, "space", split_axis=1, concat_axis=0, tiled=True)
    p1 = shifted(p0, "space", -1)
    p3 = shifted(p0, "space", -3)
    x0 = first_guess
    t0 = mm(p0, p0, 0, 0) * w[0]
    t1 = mm(p0, p1, 0, 0) * w[1]
    t3 = mm(p0, p3, 0, 0) * w[3]
    t2 = mm(p1, p3, 0, 0) * w_next[2]
    t0, t1, t2, t3 = lax.psum((t0, t1, t2, t3), "mem")
    for sweep in range(ITERS):
        x1 = shifted(x0, "space", -1)
        x3 = shifted(x0, "space", -3)
        back1 = shifted(mm(t1, x0, 0, 0) + mm(t2, x3, 1, 0), "space", 1)
        back3 = shifted(mm(t3, x0, 0, 0) + mm(t2, x1, 0, 0), "space", 3)
        own = mm(t0, x0, 1, 0) + mm(t1, x1, 1, 0) + mm(t3, x3, 1, 0)
        x0 = x0 + 0.5 * (target - x0 - (own + back1 + back3))
    return x0


def solution(mesh):
    in_specs = (
        P(("space", "mem"), None),
        P("space", None),
        P("space"),
        P(),
        P(),
        P("space", "mem"),
        P("space", "mem"),
    )
    out_specs = P("space", "mem")
    return jax.shard_map(
        per_device, mesh=mesh, in_specs=in_specs, out_specs=out_specs, check_vma=False
    )
```

```python
import jax
import jax.numpy as jnp
from jax import lax
from jax.sharding import PartitionSpec as P

BLOCK = 256
MEMBERS = 1024
REACH_DEV = 3
NBANDS = 8
ITERS = 2


def shifted(array, axis, by):
    count = lax.axis_size(axis)
    return lax.ppermute(array, axis, [(i, (i + by) % count) for i in range(count)])


def mm(a, b, ca, cb):
    return lax.dot_general(
        a, b, (((ca,), (cb,)), ((), ())), precision=lax.Precision.HIGH,
        preferred_element_type=jnp.float32,
    )


def member_sum(tile):
    if lax.axis_size("mem") == 2:
        return tile + shifted(tile, "mem", 1)
    return lax.psum(tile, "mem")


def gap_weights(pair_list, pair_count, band_weight, cov_scale):
    slots = pair_list.shape[0]
    blocks_all = lax.axis_size("space")
    gap = (pair_list[:, 1] - pair_list[:, 0]) % blocks_all
    living = (jnp.arange(slots, dtype=jnp.int32) < pair_count[0]).astype(jnp.float32)
    bands = jnp.arange(NBANDS, dtype=jnp.int32)
    band_now = jnp.sum(
        jnp.where(pair_list[:, 2][:, None] == bands[None, :], band_weight[None, :], 0.0), axis=1
    )
    slot_weight = cov_scale[0] * band_now * living / (MEMBERS - 1)
    gaps = jnp.arange(REACH_DEV + 1, dtype=jnp.int32)
    return jnp.sum(jnp.where(gap[:, None] == gaps[None, :], slot_weight[:, None], 0.0), axis=0)


def per_device(perturb, pair_list, pair_count, band_weight, cov_scale, target, first_guess):
    w = gap_weights(pair_list, pair_count, band_weight, cov_scale)
    w_next = shifted(w, "space", -1)
    p0 = lax.all_to_all(perturb, "space", split_axis=1, concat_axis=0, tiled=True)
    p1 = shifted(p0, "space", -1)
    p3 = shifted(p0, "space", -3)
    x0 = first_guess
    t0 = mm(p0, p0, 0, 0) * w[0]
    t1 = mm(p0, p1, 0, 0) * w[1]
    t3 = mm(p0, p3, 0, 0) * w[3]
    t2 = mm(p1, p3, 0, 0) * w_next[2]
    t0, t1, t2, t3 = (member_sum(t) for t in (t0, t1, t2, t3))
    for sweep in range(ITERS):
        x1 = shifted(x0, "space", -1)
        x3 = shifted(x0, "space", -3)
        back1 = shifted(mm(t1, x0, 0, 0) + mm(t2, x3, 1, 0), "space", 1)
        back3 = shifted(mm(t3, x0, 0, 0) + mm(t2, x1, 0, 0), "space", 3)
        own = mm(t0, x0, 1, 0) + mm(t1, x1, 1, 0) + mm(t3, x3, 1, 0)
        x0 = x0 + 0.5 * (target - x0 - (own + back1 + back3))
    return x0


def solution(mesh):
    in_specs = (
        P(("space", "mem"), None),
        P("space", None),
        P("space"),
        P(),
        P(),
        P("space", "mem"),
        P("space", "mem"),
    )
    out_specs = P("space", "mem")
    return jax.shard_map(
        per_device, mesh=mesh, in_specs=in_specs, out_specs=out_specs, check_vma=False
    )
```

```python
import functools
import jax
import jax.numpy as jnp
from jax import lax
from jax.experimental import pallas as pl
from jax.experimental.pallas import tpu as pltpu
from jax.sharding import PartitionSpec as P

BLOCK = 256
MEMBERS = 1024
REACH_DEV = 3
NBANDS = 8
ITERS = 2


def shifted(array, axis, by):
    count = lax.axis_size(axis)
    return lax.ppermute(array, axis, [(i, (i + by) % count) for i in range(count)])


def mm(a, b, ca, cb):
    return lax.dot_general(
        a, b, (((ca,), (cb,)), ((), ())), precision=lax.Precision.HIGH,
        preferred_element_type=jnp.float32,
    )


def member_sum(tile):
    if lax.axis_size("mem") == 2:
        return tile + shifted(tile, "mem", 1)
    return lax.psum(tile, "mem")


def gap_weights(pair_list, pair_count, band_weight, cov_scale):
    slots = pair_list.shape[0]
    blocks_all = lax.axis_size("space")
    gap = (pair_list[:, 1] - pair_list[:, 0]) % blocks_all
    living = (jnp.arange(slots, dtype=jnp.int32) < pair_count[0]).astype(jnp.float32)
    bands = jnp.arange(NBANDS, dtype=jnp.int32)
    band_now = jnp.sum(
        jnp.where(pair_list[:, 2][:, None] == bands[None, :], band_weight[None, :], 0.0), axis=1
    )
    slot_weight = cov_scale[0] * band_now * living / (MEMBERS - 1)
    gaps = jnp.arange(REACH_DEV + 1, dtype=jnp.int32)
    return jnp.sum(jnp.where(gap[:, None] == gaps[None, :], slot_weight[:, None], 0.0), axis=0)


def by_collectives(perturb, pair_list, pair_count, band_weight, cov_scale, target, first_guess):
    w = gap_weights(pair_list, pair_count, band_weight, cov_scale)
    w_next = shifted(w, "space", -1)
    p0 = lax.all_to_all(perturb, "space", split_axis=1, concat_axis=0, tiled=True)
    p1 = shifted(p0, "space", -1)
    p3 = shifted(p0, "space", -3)
    x0 = first_guess
    t0 = mm(p0, p0, 0, 0) * w[0]
    t1 = mm(p0, p1, 0, 0) * w[1]
    t3 = mm(p0, p3, 0, 0) * w[3]
    t2 = mm(p1, p3, 0, 0) * w_next[2]
    t0, t1, t2, t3 = (member_sum(t) for t in (t0, t1, t2, t3))
    for sweep in range(ITERS):
        x1 = shifted(x0, "space", -1)
        x3 = shifted(x0, "space", -3)
        back1 = shifted(mm(t1, x0, 0, 0) + mm(t2, x3, 1, 0), "space", 1)
        back3 = shifted(mm(t3, x0, 0, 0) + mm(t2, x1, 0, 0), "space", 3)
        own = mm(t0, x0, 1, 0) + mm(t1, x1, 1, 0) + mm(t3, x3, 1, 0)
        x0 = x0 + 0.5 * (target - x0 - (own + back1 + back3))
    return x0

GROUP = REACH_DEV + 1
NEAR = 2 * REACH_DEV + 1
SPANS = ((0, 0), (1, 1), (3, 2))


class Mover:
    def __init__(self, send_sem, recv_sem, local_sem):
        self.send_sem, self.recv_sem, self.local_sem = send_sem, recv_sem, local_sem
        self.sent = 0
        self.local = 0
        self.open = []

    def to(self, source, target, device):
        copy = pltpu.make_async_remote_copy(
            src_ref=source, dst_ref=target,
            send_sem=self.send_sem.at[self.sent], recv_sem=self.recv_sem.at[self.sent],
            device_id=device, device_id_type=pl.DeviceIdType.MESH,
        )
        self.sent += 1
        copy.start()
        self.open.append(copy)
        return copy

    def here(self, source, target):
        copy = pltpu.make_async_copy(source, target, self.local_sem.at[self.local])
        self.local += 1
        copy.start()
        return copy


def split(value):
    high = value.astype(jnp.bfloat16)
    return high, (value - high.astype(jnp.float32)).astype(jnp.bfloat16)


def dot(a, b, ca, cb):
    return lax.dot_general(a, b, (((ca,), (cb,)), ((), ())), preferred_element_type=jnp.float32)


def kernel(planes, perturb, table, guess, target, out, pz, pg, part, part_in, table_next, tiles,
           tile_hi, tile_lo, xb, tb, halo, xs, acc, px, ret_in, halo_in, final, send_sem, recv_sem,
           local_sem):
    space = lax.axis_index("space")
    mem = lax.axis_index("mem")
    count = planes * GROUP
    k = space // GROUP
    j = space % GROUP
    rows = perturb.shape[0]
    width = GROUP * BLOCK
    cols = xb.shape[2]
    half = BLOCK // 2

    def plane(r):
        return (((k + r) % planes) * GROUP + j, mem)

    def chip(q):
        return (k * GROUP + (j + q) % GROUP, mem)

    partner = (space, 1 - mem)
    before = ((space + count - 1) % count, mem)
    after = ((space + 1) % count, mem)
    barrier = pltpu.get_barrier_semaphore()
    greeted = [plane(r) for r in range(1, planes)] + [chip(q) for q in range(1, GROUP)]
    greeted += [partner, before, after]
    for device in greeted:
        pl.semaphore_signal(barrier, inc=1, device_id=device, device_id_type=pl.DeviceIdType.MESH)
    pl.semaphore_wait(barrier, len(greeted))

    move = Mover(send_sem, recv_sem, local_sem)

    def at(block, size):
        return pl.ds(pl.multiple_of(block * BLOCK, BLOCK), size * BLOCK)

    from_plane = {}
    for r in range(planes - 1, 0, -1):
        there = (k + planes - r) % planes
        nxt = (there + 1) % planes
        device = plane(planes - r)
        from_plane[r] = (
            move.to(perturb.at[:, at(there * GROUP, GROUP)], pz.at[r, :, pl.ds(0, width)], device),
            move.to(perturb.at[:, at(nxt * GROUP, REACH_DEV)],
                    pz.at[r, :, pl.ds(width, REACH_DEV * BLOCK)], device),
        )
    table_copy = move.to(table, table_next, before)
    own = (
        move.here(perturb.at[:, at(k * GROUP, GROUP)], pz.at[0, :, pl.ds(0, width)]),
        move.here(perturb.at[:, at(((k + 1) % planes) * GROUP, REACH_DEV)],
                  pz.at[0, :, pl.ds(width, REACH_DEV * BLOCK)]),
    )
    for copy in own:
        copy.wait()

    def spread(r):
        copies = []
        for q in range(1, GROUP):
            there = (j + q) % GROUP
            copies.append(move.to(pz.at[r, :, at(there, 2)],
                                  pg.at[r, q, :, pl.ds(0, 2 * BLOCK)], chip(q)))
            copies.append(move.to(pz.at[r, :, at(there + REACH_DEV, 1)],
                                  pg.at[r, q, :, pl.ds(2 * BLOCK, BLOCK)], chip(q)))
        mine = (move.here(pz.at[r, :, at(j, 2)], pg.at[r, 0, :, pl.ds(0, 2 * BLOCK)]),
                move.here(pz.at[r, :, at(j + REACH_DEV, 1)],
                          pg.at[r, 0, :, pl.ds(2 * BLOCK, BLOCK)]))
        return copies, mine

    def products(r, copies):
        for copy in copies[0]:
            copy.wait_recv()
        for copy in copies[1]:
            copy.wait()
        value = pg[r].reshape(GROUP * rows, 3 * BLOCK)
        high, low = split(value)
        left = jnp.concatenate([high[:, : 2 * BLOCK], high[:, : 2 * BLOCK], low[:, : 2 * BLOCK]], 0)
        right = jnp.concatenate([high, low, high], 0)
        wide = dot(left[:, :BLOCK], right, 0, 0)
        last = dot(left[:, BLOCK:], right[:, 2 * BLOCK :], 0, 0)
        if r == 0:
            part[:, : 3 * BLOCK] = wide
            part[:, 3 * BLOCK :] = last
        else:
            part[:, : 3 * BLOCK] += wide
            part[:, 3 * BLOCK :] += last

    spreading = {0: spread(0)}

    def share(source, blocks):
        copies = []
        for q in range(1, GROUP):
            there = (j + q) % GROUP
            piece = source.at[:, pl.ds(pl.multiple_of(there * cols, cols), cols)]
            copies.append(move.to(piece, blocks.at[j], chip(q)))
        mine = move.here(source.at[:, pl.ds(pl.multiple_of(j * cols, cols), cols)], blocks.at[j])
        return copies, mine

    guesses = share(guess, xb)
    targets = share(target, tb)
    order = list(range(1, planes))
    for r in order:
        for copy in from_plane[r]:
            copy.wait_recv()
        spreading[r] = spread(r)
        products(r - 1, spreading[r - 1])
    for copy in guesses[0]:
        copy.wait_recv()
    guesses[1].wait()
    halo_copy = move.to(xb.at[pl.ds(0, REACH_DEV)], halo, plane(planes - 1))
    for n in range(GROUP):
        xs[n, :, :cols], xs[n, :, cols:] = split(xb[n])
    products(planes - 1, spreading[planes - 1])

    mine = pl.ds(pl.multiple_of(mem * half, half), half)
    other = pl.ds(pl.multiple_of((1 - mem) * half, half), half)
    part_copy = move.to(part.at[other], part_in, partner)
    table_copy.wait_recv()
    part_copy.wait_recv()
    rates = (table[0:1], table[1:2], table[3:4], table_next[2:3])
    for n, rate in enumerate(rates):
        span = pl.ds(n * BLOCK, BLOCK)
        tiles[j, mine, span] = (part[mine, span] + part_in[:, span]) * rate
    gather = {q: move.to(tiles.at[j, mine], tiles.at[j, mine], chip(q)) for q in range(1, GROUP)}
    pair = {0: move.to(tiles.at[j, mine], tiles.at[j, mine], partner)}

    halo_copy.wait_recv()
    for n in range(REACH_DEV):
        xs[GROUP + n, :, :cols], xs[GROUP + n, :, cols:] = split(halo[n])
    for n in range(NEAR):
        acc[0, n] = jnp.zeros_like(acc[0, n])
        acc[1, n] = jnp.zeros_like(acc[1, n])

    def times(high, low, x, side):
        both = dot(high, x, side, 0)
        return both[:, :cols] + both[:, cols:] + dot(low, x[:, :cols], side, 0)

    def apply(sweep, i):
        xa, xb_, xc = xs[i], xs[i + 1], xs[i + 3]
        high, low = tile_hi[i], tile_lo[i]
        B = BLOCK
        acc[sweep, i] += (times(high[:, :B], low[:, :B], xa, 1)
                          + times(high[:, B : 2 * B], low[:, B : 2 * B], xb_, 1)
                          + times(high[:, 2 * B : 3 * B], low[:, 2 * B : 3 * B], xc, 1))
        down = times(high[:, B : 3 * B], low[:, B : 3 * B], xa, 0)
        acc[sweep, i + 1] += down[:B] + times(high[:, 3 * B :], low[:, 3 * B :], xc, 1)
        acc[sweep, i + 3] += down[B:] + times(high[:, 3 * B :], low[:, 3 * B :], xb_, 0)

    for q in range(GROUP):
        i = (j + GROUP - q) % GROUP
        if q + 1 < GROUP:
            gather[q + 1].wait_recv()
            there = (j + GROUP - q - 1) % GROUP
            pair[q + 1] = move.to(tiles.at[there, mine], tiles.at[there, mine], partner)
        pair[q].wait_recv()
        tile_hi[i], tile_lo[i] = split(tiles[i])
        apply(0, i)

    for copy in targets[0]:
        copy.wait_recv()
    targets[1].wait()
    back = move.to(acc.at[0, pl.ds(GROUP, REACH_DEV)], ret_in.at[0], plane(1))
    for n in range(GROUP):
        px[n] = xb[n] + 0.5 * (tb[n] - xb[n] - acc[0, n])
    ahead = move.to(px.at[pl.ds(0, REACH_DEV)], halo_in, plane(planes - 1))
    final[GROUP - 1] = px[GROUP - 1]
    xs[GROUP - 1, :, :cols], xs[GROUP - 1, :, cols:] = split(px[GROUP - 1])
    back.wait_recv()
    for n in range(REACH_DEV):
        now = px[n] - 0.5 * ret_in[0, n]
        final[n] = now
        xs[n, :, :cols], xs[n, :, cols:] = split(now)
    ahead.wait_recv()
    for n in range(REACH_DEV):
        now = halo_in[n] - 0.5 * acc[0, GROUP + n]
        xs[GROUP + n, :, :cols], xs[GROUP + n, :, cols:] = split(now)

    @pl.loop(0, GROUP)
    def _(step):
        apply(1, step)

    back = move.to(acc.at[1, pl.ds(GROUP, REACH_DEV)], ret_in.at[1], plane(1))
    for n in range(GROUP):
        now = final[n]
        final[n] = now + 0.5 * (tb[n] - now - acc[1, n])
    back.wait_recv()
    for n in range(REACH_DEV):
        final[n] = final[n] - 0.5 * ret_in[1, n]
    place = pl.ds(pl.multiple_of(j * cols, cols), cols)
    done = []
    for q in range(1, GROUP):
        there = (j + q) % GROUP
        done.append(move.to(final.at[there], out.at[:, place], chip(q)))
    last = move.here(final.at[j], out.at[:, place])
    for copy in done:
        copy.wait_recv()
    last.wait()
    for copy in move.open:
        copy.wait_send()


def in_one_kernel(perturb, pair_list, pair_count, band_weight, cov_scale, target, first_guess):
    w = gap_weights(pair_list, pair_count, band_weight, cov_scale)
    table = jnp.broadcast_to(jnp.pad(w, (0, 8 - w.shape[0]))[:, None], (8, BLOCK))
    planes = lax.axis_size("space") // GROUP
    rows = perturb.shape[0]
    cols = first_guess.shape[1] // GROUP
    f32, bf16 = jnp.float32, jnp.bfloat16
    sends = 2 * (planes - 1) + 1 + planes * 2 * (GROUP - 1) + 2 * (GROUP - 1) + 1 + 1
    sends += 2 * (GROUP - 1) + 1 + 3 + GROUP - 1
    locals_ = 2 + 2 * planes + 2 + 1
    vmem = pl.BlockSpec(memory_space=pltpu.VMEM)
    return pl.pallas_call(
        functools.partial(kernel, planes),
        out_shape=jax.ShapeDtypeStruct(first_guess.shape, f32),
        in_specs=[vmem] * 4,
        out_specs=vmem,
        scratch_shapes=[
            pltpu.VMEM((planes, rows, NEAR * BLOCK), f32),
            pltpu.VMEM((planes, GROUP, rows, 3 * BLOCK), f32),
            pltpu.VMEM((BLOCK, 4 * BLOCK), f32),
            pltpu.VMEM((BLOCK // 2, 4 * BLOCK), f32),
            pltpu.VMEM((8, BLOCK), f32),
            pltpu.VMEM((GROUP, BLOCK, 4 * BLOCK), f32),
            pltpu.VMEM((GROUP, BLOCK, 4 * BLOCK), bf16),
            pltpu.VMEM((GROUP, BLOCK, 4 * BLOCK), bf16),
            pltpu.VMEM((GROUP, BLOCK, cols), f32),
            pltpu.VMEM((GROUP, BLOCK, cols), f32),
            pltpu.VMEM((REACH_DEV, BLOCK, cols), f32),
            pltpu.VMEM((NEAR, BLOCK, 2 * cols), bf16),
            pltpu.VMEM((2, NEAR, BLOCK, cols), f32),
            pltpu.VMEM((GROUP, BLOCK, cols), f32),
            pltpu.VMEM((2, REACH_DEV, BLOCK, cols), f32),
            pltpu.VMEM((REACH_DEV, BLOCK, cols), f32),
            pltpu.VMEM((GROUP, BLOCK, cols), f32),
            pltpu.SemaphoreType.DMA((sends,)),
            pltpu.SemaphoreType.DMA((sends,)),
            pltpu.SemaphoreType.DMA((locals_,)),
        ],
        compiler_params=pltpu.CompilerParams(
            collective_id=0, has_side_effects=True, vmem_limit_bytes=48 * 1024 * 1024
        ),
    )(perturb, table, first_guess, target)


def fits(perturb, field):
    planes, rest = divmod(lax.axis_size("space"), GROUP)
    return (
        lax.axis_size("mem") == 2 and rest == 0 and planes >= 2
        and perturb.shape[0] % 8 == 0 and field.shape[1] % (GROUP * 128) == 0
        and field.shape[0] == BLOCK
    )


def per_device(perturb, pair_list, pair_count, band_weight, cov_scale, target, first_guess):
    whole = in_one_kernel if fits(perturb, first_guess) else by_collectives
    return whole(perturb, pair_list, pair_count, band_weight, cov_scale, target, first_guess)


def solution(mesh):
    in_specs = (
        P(("space", "mem"), None),
        P("space", None),
        P("space"),
        P(),
        P(),
        P("space", "mem"),
        P("space", "mem"),
    )
    out_specs = P("space", "mem")
    return jax.shard_map(
        per_device, mesh=mesh, in_specs=in_specs, out_specs=out_specs, check_vma=False
    )
```

```python
import functools
import jax
import jax.numpy as jnp
from jax import lax
from jax.experimental import pallas as pl
from jax.experimental.pallas import tpu as pltpu
from jax.sharding import PartitionSpec as P

BLOCK = 256
MEMBERS = 1024
REACH_DEV = 3
NBANDS = 8
ITERS = 2


def shifted(array, axis, by):
    count = lax.axis_size(axis)
    return lax.ppermute(array, axis, [(i, (i + by) % count) for i in range(count)])


def mm(a, b, ca, cb):
    return lax.dot_general(
        a, b, (((ca,), (cb,)), ((), ())), precision=lax.Precision.HIGH,
        preferred_element_type=jnp.float32,
    )


def member_sum(tile):
    if lax.axis_size("mem") == 2:
        return tile + shifted(tile, "mem", 1)
    return lax.psum(tile, "mem")


def gap_weights(pair_list, pair_count, band_weight, cov_scale):
    slots = pair_list.shape[0]
    blocks_all = lax.axis_size("space")
    gap = (pair_list[:, 1] - pair_list[:, 0]) % blocks_all
    living = (jnp.arange(slots, dtype=jnp.int32) < pair_count[0]).astype(jnp.float32)
    bands = jnp.arange(NBANDS, dtype=jnp.int32)
    band_now = jnp.sum(
        jnp.where(pair_list[:, 2][:, None] == bands[None, :], band_weight[None, :], 0.0), axis=1
    )
    slot_weight = cov_scale[0] * band_now * living / (MEMBERS - 1)
    gaps = jnp.arange(REACH_DEV + 1, dtype=jnp.int32)
    return jnp.sum(jnp.where(gap[:, None] == gaps[None, :], slot_weight[:, None], 0.0), axis=0)


def by_collectives(perturb, pair_list, pair_count, band_weight, cov_scale, target, first_guess):
    w = gap_weights(pair_list, pair_count, band_weight, cov_scale)
    w_next = shifted(w, "space", -1)
    p0 = lax.all_to_all(perturb, "space", split_axis=1, concat_axis=0, tiled=True)
    p1 = shifted(p0, "space", -1)
    p3 = shifted(p0, "space", -3)
    x0 = first_guess
    t0 = mm(p0, p0, 0, 0) * w[0]
    t1 = mm(p0, p1, 0, 0) * w[1]
    t3 = mm(p0, p3, 0, 0) * w[3]
    t2 = mm(p1, p3, 0, 0) * w_next[2]
    t0, t1, t2, t3 = (member_sum(t) for t in (t0, t1, t2, t3))
    for sweep in range(ITERS):
        x1 = shifted(x0, "space", -1)
        x3 = shifted(x0, "space", -3)
        back1 = shifted(mm(t1, x0, 0, 0) + mm(t2, x3, 1, 0), "space", 1)
        back3 = shifted(mm(t3, x0, 0, 0) + mm(t2, x1, 0, 0), "space", 3)
        own = mm(t0, x0, 1, 0) + mm(t1, x1, 1, 0) + mm(t3, x3, 1, 0)
        x0 = x0 + 0.5 * (target - x0 - (own + back1 + back3))
    return x0

GROUP = REACH_DEV + 1
NEAR = 2 * REACH_DEV + 1
SPANS = ((0, 0), (1, 1), (3, 2))


class Mover:
    def __init__(self, send_sem, recv_sem, local_sem):
        self.send_sem, self.recv_sem, self.local_sem = send_sem, recv_sem, local_sem
        self.sent = 0
        self.local = 0
        self.open = []

    def to(self, source, target, device):
        copy = pltpu.make_async_remote_copy(
            src_ref=source, dst_ref=target,
            send_sem=self.send_sem.at[self.sent], recv_sem=self.recv_sem.at[self.sent],
            device_id=device, device_id_type=pl.DeviceIdType.MESH,
        )
        self.sent += 1
        copy.start()
        self.open.append(copy)
        return copy

    def here(self, source, target):
        copy = pltpu.make_async_copy(source, target, self.local_sem.at[self.local])
        self.local += 1
        copy.start()
        return copy


def split(value):
    high = value.astype(jnp.bfloat16)
    return high, (value - high.astype(jnp.float32)).astype(jnp.bfloat16)


def dot(a, b, ca, cb):
    return lax.dot_general(a, b, (((ca,), (cb,)), ((), ())), preferred_element_type=jnp.float32)


def kernel(planes, perturb, table, guess, target, out, pz, pg, part, part_in, table_next, tiles,
           tile_hi, tile_lo, xb, tb, halo, xs, acc, px, ret_in, halo_in, final, send_sem, recv_sem,
           local_sem):
    space = lax.axis_index("space")
    mem = lax.axis_index("mem")
    count = planes * GROUP
    k = space // GROUP
    j = space % GROUP
    rows = perturb.shape[0]
    width = GROUP * BLOCK
    cols = xb.shape[2]
    half = BLOCK // 2

    def plane(r):
        return (((k + r) % planes) * GROUP + j, mem)

    def chip(q):
        return (k * GROUP + (j + q) % GROUP, mem)

    partner = (space, 1 - mem)
    before = ((space + count - 1) % count, mem)
    after = ((space + 1) % count, mem)
    barrier = pltpu.get_barrier_semaphore()
    greeted = [plane(r) for r in range(1, planes)] + [chip(q) for q in range(1, GROUP)]
    greeted += [partner, before, after]
    for device in greeted:
        pl.semaphore_signal(barrier, inc=1, device_id=device, device_id_type=pl.DeviceIdType.MESH)
    pl.semaphore_wait(barrier, len(greeted))

    move = Mover(send_sem, recv_sem, local_sem)

    def at(block, size):
        return pl.ds(pl.multiple_of(block * BLOCK, BLOCK), size * BLOCK)

    from_plane = {}
    for r in range(planes - 1, 0, -1):
        there = (k + planes - r) % planes
        nxt = (there + 1) % planes
        device = plane(planes - r)
        from_plane[r] = (
            move.to(perturb.at[:, at(there * GROUP, GROUP)], pz.at[r, :, pl.ds(0, width)], device),
            move.to(perturb.at[:, at(nxt * GROUP, REACH_DEV)],
                    pz.at[r, :, pl.ds(width, REACH_DEV * BLOCK)], device),
        )
    table_copy = move.to(table, table_next, before)
    own = (
        move.here(perturb.at[:, at(k * GROUP, GROUP)], pz.at[0, :, pl.ds(0, width)]),
        move.here(perturb.at[:, at(((k + 1) % planes) * GROUP, REACH_DEV)],
                  pz.at[0, :, pl.ds(width, REACH_DEV * BLOCK)]),
    )
    for copy in own:
        copy.wait()

    def spread(r):
        copies = []
        for q in range(1, GROUP):
            there = (j + q) % GROUP
            copies.append(move.to(pz.at[r, :, at(there, 2)],
                                  pg.at[r, q, :, pl.ds(0, 2 * BLOCK)], chip(q)))
            copies.append(move.to(pz.at[r, :, at(there + REACH_DEV, 1)],
                                  pg.at[r, q, :, pl.ds(2 * BLOCK, BLOCK)], chip(q)))
        mine = (move.here(pz.at[r, :, at(j, 2)], pg.at[r, 0, :, pl.ds(0, 2 * BLOCK)]),
                move.here(pz.at[r, :, at(j + REACH_DEV, 1)],
                          pg.at[r, 0, :, pl.ds(2 * BLOCK, BLOCK)]))
        return copies, mine

    def products(r, copies):
        for copy in copies[0]:
            copy.wait_recv()
        for copy in copies[1]:
            copy.wait()
        value = pg[r].reshape(GROUP * rows, 3 * BLOCK)
        high, low = split(value)
        left = jnp.concatenate([high[:, : 2 * BLOCK], high[:, : 2 * BLOCK], low[:, : 2 * BLOCK]], 0)
        right = jnp.concatenate([high, low, high], 0)
        wide = dot(left[:, :BLOCK], right, 0, 0)
        last = dot(left[:, BLOCK:], right[:, 2 * BLOCK :], 0, 0)
        if r == 0:
            part[:, : 3 * BLOCK] = wide
            part[:, 3 * BLOCK :] = last
        else:
            part[:, : 3 * BLOCK] += wide
            part[:, 3 * BLOCK :] += last

    spreading = {0: spread(0)}

    def share(source, blocks):
        copies = []
        for q in range(1, GROUP):
            there = (j + q) % GROUP
            piece = source.at[:, pl.ds(pl.multiple_of(there * cols, cols), cols)]
            copies.append(move.to(piece, blocks.at[j], chip(q)))
        mine = move.here(source.at[:, pl.ds(pl.multiple_of(j * cols, cols), cols)], blocks.at[j])
        return copies, mine

    guesses = share(guess, xb)
    targets = share(target, tb)
    order = list(range(1, planes))
    for r in order:
        for copy in from_plane[r]:
            copy.wait_recv()
        spreading[r] = spread(r)
        products(r - 1, spreading[r - 1])
    for copy in guesses[0]:
        copy.wait_recv()
    guesses[1].wait()
    halo_copy = move.to(xb.at[pl.ds(0, REACH_DEV)], halo, plane(planes - 1))
    for n in range(GROUP):
        xs[n, :, :cols], xs[n, :, cols:] = split(xb[n])
    products(planes - 1, spreading[planes - 1])

    mine = pl.ds(pl.multiple_of(mem * half, half), half)
    other = pl.ds(pl.multiple_of((1 - mem) * half, half), half)
    part_copy = move.to(part.at[other], part_in, partner)
    table_copy.wait_recv()
    part_copy.wait_recv()
    rates = (table[0:1], table[1:2], table[3:4], table_next[2:3])
    for n, rate in enumerate(rates):
        span = pl.ds(n * BLOCK, BLOCK)
        tiles[j, mine, span] = (part[mine, span] + part_in[:, span]) * rate
    side = j + 1 - 2 * (j % 2)
    over = (j + 2) % GROUP
    far = (side + 2) % GROUP

    def tile_to(i, device):
        return move.to(tiles.at[i, mine], tiles.at[i, mine], device)

    near_copies = [tile_to(j, (k * GROUP + there, mem)) for there in (side, over)]
    pair = {0: tile_to(j, partner)}

    halo_copy.wait_recv()
    for n in range(REACH_DEV):
        xs[GROUP + n, :, :cols], xs[GROUP + n, :, cols:] = split(halo[n])
    for n in range(NEAR):
        acc[0, n] = jnp.zeros_like(acc[0, n])
        acc[1, n] = jnp.zeros_like(acc[1, n])

    def times(high, low, x, side):
        both = dot(high, x, side, 0)
        return both[:, :cols] + both[:, cols:] + dot(low, x[:, :cols], side, 0)

    def apply(sweep, i):
        xa, xb_, xc = xs[i], xs[i + 1], xs[i + 3]
        high, low = tile_hi[i], tile_lo[i]
        B = BLOCK
        acc[sweep, i] += (times(high[:, :B], low[:, :B], xa, 1)
                          + times(high[:, B : 2 * B], low[:, B : 2 * B], xb_, 1)
                          + times(high[:, 2 * B : 3 * B], low[:, 2 * B : 3 * B], xc, 1))
        down = times(high[:, B : 3 * B], low[:, B : 3 * B], xa, 0)
        acc[sweep, i + 1] += down[:B] + times(high[:, 3 * B :], low[:, 3 * B :], xc, 1)
        acc[sweep, i + 3] += down[B:] + times(high[:, 3 * B :], low[:, 3 * B :], xb_, 0)

    def take(step, i):
        pair[step].wait_recv()
        tile_hi[i], tile_lo[i] = split(tiles[i])
        apply(0, i)

    take(0, j)
    for copy in near_copies:
        copy.wait_recv()
    onward = tile_to(side + mem * (over - side), (k * GROUP + over + mem * (side - over), mem))
    pair[1] = tile_to(side, partner)
    pair[2] = tile_to(over, partner)
    take(1, side)
    take(2, over)
    onward.wait_recv()
    pair[3] = tile_to(far, partner)
    take(3, far)

    for copy in targets[0]:
        copy.wait_recv()
    targets[1].wait()
    def back(sweep, n):
        return move.to(acc.at[sweep, GROUP + n], ret_in.at[sweep, n], plane(1))

    backs = [back(0, n) for n in range(2)]
    aheads = []
    for n in range(GROUP):
        px[n] = xb[n] + 0.5 * (tb[n] - xb[n] - acc[0, n])
        if n < REACH_DEV:
            aheads.append(move.to(px.at[n], halo_in.at[n], plane(planes - 1)))
    backs.append(back(0, 2))

    def settle(n, now):
        xs[n, :, :cols], xs[n, :, cols:] = split(now)
        if n < GROUP:
            final[n] = now + 0.5 * (tb[n] - now)

    def settle_own(n):
        backs[n].wait_recv()
        settle(n, px[n] - 0.5 * ret_in[0, n])

    def settle_halo(n):
        aheads[n].wait_recv()
        settle(GROUP + n, halo_in[n] - 0.5 * acc[0, GROUP + n])

    place = pl.ds(pl.multiple_of(j * cols, cols), cols)
    base = move.sent
    here_sem = local_sem.at[move.local]

    def leave(n, source):
        return pltpu.make_async_remote_copy(
            src_ref=final.at[n], dst_ref=out.at[:, place],
            send_sem=send_sem.at[base + n], recv_sem=recv_sem.at[base + source],
            device_id=(k * GROUP + n, mem), device_id_type=pl.DeviceIdType.MESH,
        )

    def stay(n):
        return pltpu.make_async_copy(final.at[n], out.at[:, place], here_sem)

    def put(n):
        @pl.when(j != n)
        def _():
            leave(n, j).start()

        @pl.when(j == n)
        def _():
            stay(n).start()

    move.sent = base + GROUP
    settle(GROUP - 1, px[GROUP - 1])
    settle_own(0)
    settle_own(1)
    apply(1, 0)
    settle_own(2)
    settle_halo(0)
    apply(1, 1)
    settle_halo(1)
    apply(1, 2)
    backs = {1: back(1, 1)}
    settle_halo(2)
    apply(1, 3)
    backs[0] = back(1, 0)
    backs[2] = back(1, 2)
    final[3] = final[3] - 0.5 * acc[1, 3]
    put(3)
    for n in (1, 0, 2):
        backs[n].wait_recv()
        final[n] = final[n] - 0.5 * (acc[1, n] + ret_in[1, n])
        put(n)
    for n in range(GROUP):
        @pl.when(j != n)
        def _():
            leave(n, n).wait_send()
            leave(n, n).wait_recv()

        @pl.when(j == n)
        def _():
            stay(n).wait()
    for copy in move.open:
        copy.wait_send()


def in_one_kernel(perturb, pair_list, pair_count, band_weight, cov_scale, target, first_guess):
    w = gap_weights(pair_list, pair_count, band_weight, cov_scale)
    table = jnp.broadcast_to(jnp.pad(w, (0, 8 - w.shape[0]))[:, None], (8, BLOCK))
    planes = lax.axis_size("space") // GROUP
    rows = perturb.shape[0]
    cols = first_guess.shape[1] // GROUP
    f32, bf16 = jnp.float32, jnp.bfloat16
    sends = 2 * (planes - 1) + 1 + planes * 2 * (GROUP - 1) + 2 * (GROUP - 1) + 1 + 1
    sends += 3 + GROUP + 1 + 3 * REACH_DEV + GROUP
    locals_ = 2 + 2 * planes + 2 + 1
    vmem = pl.BlockSpec(memory_space=pltpu.VMEM)
    return pl.pallas_call(
        functools.partial(kernel, planes),
        out_shape=jax.ShapeDtypeStruct(first_guess.shape, f32),
        in_specs=[vmem] * 4,
        out_specs=vmem,
        scratch_shapes=[
            pltpu.VMEM((planes, rows, NEAR * BLOCK), f32),
            pltpu.VMEM((planes, GROUP, rows, 3 * BLOCK), f32),
            pltpu.VMEM((BLOCK, 4 * BLOCK), f32),
            pltpu.VMEM((BLOCK // 2, 4 * BLOCK), f32),
            pltpu.VMEM((8, BLOCK), f32),
            pltpu.VMEM((GROUP, BLOCK, 4 * BLOCK), f32),
            pltpu.VMEM((GROUP, BLOCK, 4 * BLOCK), bf16),
            pltpu.VMEM((GROUP, BLOCK, 4 * BLOCK), bf16),
            pltpu.VMEM((GROUP, BLOCK, cols), f32),
            pltpu.VMEM((GROUP, BLOCK, cols), f32),
            pltpu.VMEM((REACH_DEV, BLOCK, cols), f32),
            pltpu.VMEM((NEAR, BLOCK, 2 * cols), bf16),
            pltpu.VMEM((2, NEAR, BLOCK, cols), f32),
            pltpu.VMEM((GROUP, BLOCK, cols), f32),
            pltpu.VMEM((2, REACH_DEV, BLOCK, cols), f32),
            pltpu.VMEM((REACH_DEV, BLOCK, cols), f32),
            pltpu.VMEM((GROUP, BLOCK, cols), f32),
            pltpu.SemaphoreType.DMA((sends,)),
            pltpu.SemaphoreType.DMA((sends,)),
            pltpu.SemaphoreType.DMA((locals_,)),
        ],
        compiler_params=pltpu.CompilerParams(
            collective_id=0, has_side_effects=True, vmem_limit_bytes=48 * 1024 * 1024
        ),
    )(perturb, table, first_guess, target)


def fits(perturb, field):
    planes, rest = divmod(lax.axis_size("space"), GROUP)
    return (
        lax.axis_size("mem") == 2 and rest == 0 and planes >= 2
        and perturb.shape[0] % 8 == 0 and field.shape[1] % (GROUP * 128) == 0
        and field.shape[0] == BLOCK
    )


def per_device(perturb, pair_list, pair_count, band_weight, cov_scale, target, first_guess):
    whole = in_one_kernel if fits(perturb, first_guess) else by_collectives
    return whole(perturb, pair_list, pair_count, band_weight, cov_scale, target, first_guess)


def solution(mesh):
    in_specs = (
        P(("space", "mem"), None),
        P("space", None),
        P("space"),
        P(),
        P(),
        P("space", "mem"),
        P("space", "mem"),
    )
    out_specs = P("space", "mem")
    return jax.shard_map(
        per_device, mesh=mesh, in_specs=in_specs, out_specs=out_specs, check_vma=False
    )
```

```python
import functools
import jax
import jax.numpy as jnp
from jax import lax
from jax.experimental import pallas as pl
from jax.experimental.pallas import tpu as pltpu
from jax.sharding import PartitionSpec as P

BLOCK = 256
MEMBERS = 1024
REACH_DEV = 3
NBANDS = 8
ITERS = 2


def shifted(array, axis, by):
    count = lax.axis_size(axis)
    return lax.ppermute(array, axis, [(i, (i + by) % count) for i in range(count)])


def mm(a, b, ca, cb):
    return lax.dot_general(
        a, b, (((ca,), (cb,)), ((), ())), precision=lax.Precision.HIGH,
        preferred_element_type=jnp.float32,
    )


def member_sum(tile):
    if lax.axis_size("mem") == 2:
        return tile + shifted(tile, "mem", 1)
    return lax.psum(tile, "mem")


def gap_weights(pair_list, pair_count, band_weight, cov_scale):
    slots = pair_list.shape[0]
    blocks_all = lax.axis_size("space")
    gap = (pair_list[:, 1] - pair_list[:, 0]) % blocks_all
    living = (jnp.arange(slots, dtype=jnp.int32) < pair_count[0]).astype(jnp.float32)
    bands = jnp.arange(NBANDS, dtype=jnp.int32)
    band_now = jnp.sum(
        jnp.where(pair_list[:, 2][:, None] == bands[None, :], band_weight[None, :], 0.0), axis=1
    )
    slot_weight = cov_scale[0] * band_now * living / (MEMBERS - 1)
    gaps = jnp.arange(REACH_DEV + 1, dtype=jnp.int32)
    return jnp.sum(jnp.where(gap[:, None] == gaps[None, :], slot_weight[:, None], 0.0), axis=0)


def by_collectives(perturb, pair_list, pair_count, band_weight, cov_scale, target, first_guess):
    w = gap_weights(pair_list, pair_count, band_weight, cov_scale)
    w_next = shifted(w, "space", -1)
    p0 = lax.all_to_all(perturb, "space", split_axis=1, concat_axis=0, tiled=True)
    p1 = shifted(p0, "space", -1)
    p3 = shifted(p0, "space", -3)
    x0 = first_guess
    t0 = mm(p0, p0, 0, 0) * w[0]
    t1 = mm(p0, p1, 0, 0) * w[1]
    t3 = mm(p0, p3, 0, 0) * w[3]
    t2 = mm(p1, p3, 0, 0) * w_next[2]
    t0, t1, t2, t3 = (member_sum(t) for t in (t0, t1, t2, t3))
    for sweep in range(ITERS):
        x1 = shifted(x0, "space", -1)
        x3 = shifted(x0, "space", -3)
        back1 = shifted(mm(t1, x0, 0, 0) + mm(t2, x3, 1, 0), "space", 1)
        back3 = shifted(mm(t3, x0, 0, 0) + mm(t2, x1, 0, 0), "space", 3)
        own = mm(t0, x0, 1, 0) + mm(t1, x1, 1, 0) + mm(t3, x3, 1, 0)
        x0 = x0 + 0.5 * (target - x0 - (own + back1 + back3))
    return x0

GROUP = REACH_DEV + 1
NEAR = 2 * REACH_DEV + 1
SPANS = ((0, 0), (1, 1), (3, 2))


class Mover:
    def __init__(self, send_sem, recv_sem, local_sem):
        self.send_sem, self.recv_sem, self.local_sem = send_sem, recv_sem, local_sem
        self.sent = 0
        self.local = 0
        self.open = []

    def to(self, source, target, device):
        copy = pltpu.make_async_remote_copy(
            src_ref=source, dst_ref=target,
            send_sem=self.send_sem.at[self.sent], recv_sem=self.recv_sem.at[self.sent],
            device_id=device, device_id_type=pl.DeviceIdType.MESH,
        )
        self.sent += 1
        copy.start()
        self.open.append(copy)
        return copy

    def here(self, source, target):
        copy = pltpu.make_async_copy(source, target, self.local_sem.at[self.local])
        self.local += 1
        copy.start()
        return copy


def split(value):
    high = value.astype(jnp.bfloat16)
    return high, (value - high.astype(jnp.float32)).astype(jnp.bfloat16)


def dot(a, b, ca, cb):
    return lax.dot_general(a, b, (((ca,), (cb,)), ((), ())), preferred_element_type=jnp.float32)


def kernel(planes, perturb, table, guess, target, out, pz, pg, part, part_in, table_next, tiles,
           tile_hi, tile_lo, xb, tb, halo, xs, acc, px, ret_in, halo_in, final, send_sem, recv_sem,
           local_sem):
    space = lax.axis_index("space")
    mem = lax.axis_index("mem")
    count = planes * GROUP
    k = space // GROUP
    j = space % GROUP
    rows = perturb.shape[0]
    width = GROUP * BLOCK
    cols = xb.shape[2]
    half = BLOCK // 2

    def plane(r):
        return (((k + r) % planes) * GROUP + j, mem)

    def chip(q):
        return (k * GROUP + (j + q) % GROUP, mem)

    partner = (space, 1 - mem)
    before = ((space + count - 1) % count, mem)
    after = ((space + 1) % count, mem)
    barrier = pltpu.get_barrier_semaphore()
    greeted = [plane(r) for r in range(1, planes)] + [chip(q) for q in range(1, GROUP)]
    greeted += [partner, before, after]
    for device in greeted:
        pl.semaphore_signal(barrier, inc=1, device_id=device, device_id_type=pl.DeviceIdType.MESH)
    pl.semaphore_wait(barrier, len(greeted))

    move = Mover(send_sem, recv_sem, local_sem)

    def at(block, size):
        return pl.ds(pl.multiple_of(block * BLOCK, BLOCK), size * BLOCK)

    from_plane = {}
    for r in range(planes - 1, 0, -1):
        there = (k + planes - r) % planes
        nxt = (there + 1) % planes
        device = plane(planes - r)
        from_plane[r] = (
            move.to(perturb.at[:, at(there * GROUP, GROUP)], pz.at[r, :, pl.ds(0, width)], device),
            move.to(perturb.at[:, at(nxt * GROUP, REACH_DEV)],
                    pz.at[r, :, pl.ds(width, REACH_DEV * BLOCK)], device),
        )
    table_copy = move.to(table, table_next, before)
    own = (
        move.here(perturb.at[:, at(k * GROUP, GROUP)], pz.at[0, :, pl.ds(0, width)]),
        move.here(perturb.at[:, at(((k + 1) % planes) * GROUP, REACH_DEV)],
                  pz.at[0, :, pl.ds(width, REACH_DEV * BLOCK)]),
    )
    for copy in own:
        copy.wait()

    def spread(r):
        copies = []
        for q in range(1, GROUP):
            there = (j + q) % GROUP
            copies.append(move.to(pz.at[r, :, at(there, 2)],
                                  pg.at[r, q, :, pl.ds(0, 2 * BLOCK)], chip(q)))
            copies.append(move.to(pz.at[r, :, at(there + REACH_DEV, 1)],
                                  pg.at[r, q, :, pl.ds(2 * BLOCK, BLOCK)], chip(q)))
        mine = (move.here(pz.at[r, :, at(j, 2)], pg.at[r, 0, :, pl.ds(0, 2 * BLOCK)]),
                move.here(pz.at[r, :, at(j + REACH_DEV, 1)],
                          pg.at[r, 0, :, pl.ds(2 * BLOCK, BLOCK)]))
        return copies, mine

    def arrive(copies):
        for copy in copies[0]:
            copy.wait_recv()
        for copy in copies[1]:
            copy.wait()

    def products(r):
        value = pg[r].reshape(GROUP * rows, 3 * BLOCK)
        high, low = split(value)
        left = jnp.concatenate([high[:, : 2 * BLOCK], high[:, : 2 * BLOCK], low[:, : 2 * BLOCK]], 0)
        right = jnp.concatenate([high, low, high], 0)
        wide = dot(left[:, :BLOCK], right, 0, 0)
        last = dot(left[:, BLOCK:], right[:, 2 * BLOCK :], 0, 0)
        if r == 0:
            part[:, : 3 * BLOCK] = wide
            part[:, 3 * BLOCK :] = last
        else:
            part[:, : 3 * BLOCK] += wide
            part[:, 3 * BLOCK :] += last

    spreading = {0: spread(0)}

    def share(source, blocks):
        copies = []
        for q in range(1, GROUP):
            there = (j + q) % GROUP
            piece = source.at[:, pl.ds(pl.multiple_of(there * cols, cols), cols)]
            copies.append(move.to(piece, blocks.at[j], chip(q)))
        mine = move.here(source.at[:, pl.ds(pl.multiple_of(j * cols, cols), cols)], blocks.at[j])
        return copies, mine

    guesses = share(guess, xb)
    order = list(range(1, planes))
    for r in order:
        for copy in from_plane[r]:
            copy.wait_recv()
        spreading[r] = spread(r)
        arrive(spreading[r - 1])
        products(r - 1)
    for copy in guesses[0]:
        copy.wait_recv()
    guesses[1].wait()
    halo_copy = move.to(xb.at[pl.ds(0, REACH_DEV)], halo, plane(planes - 1))
    for n in range(GROUP):
        xs[n, :, :cols], xs[n, :, cols:] = split(xb[n])
    arrive(spreading[planes - 1])
    targets = share(target, tb)
    products(planes - 1)

    mine = pl.ds(pl.multiple_of(mem * half, half), half)
    other = pl.ds(pl.multiple_of((1 - mem) * half, half), half)
    part_copy = move.to(part.at[other], part_in, partner)
    table_copy.wait_recv()
    part_copy.wait_recv()
    rates = (table[0:1], table[1:2], table[3:4], table_next[2:3])
    for n, rate in enumerate(rates):
        span = pl.ds(n * BLOCK, BLOCK)
        tiles[j, mine, span] = (part[mine, span] + part_in[:, span]) * rate
    side = j + 1 - 2 * (j % 2)
    over = (j + 2) % GROUP
    far = (side + 2) % GROUP

    def tile_to(i, device):
        return move.to(tiles.at[i, mine], tiles.at[i, mine], device)

    near_copies = [tile_to(j, (k * GROUP + there, mem)) for there in (side, over)]
    pair = {0: tile_to(j, partner)}

    halo_copy.wait_recv()
    for n in range(REACH_DEV):
        xs[GROUP + n, :, :cols], xs[GROUP + n, :, cols:] = split(halo[n])
    for n in range(NEAR):
        acc[0, n] = jnp.zeros_like(acc[0, n])
        acc[1, n] = jnp.zeros_like(acc[1, n])

    def times(high, low, x, side):
        both = dot(high, x, side, 0)
        return both[:, :cols] + both[:, cols:] + dot(low, x[:, :cols], side, 0)

    def apply(sweep, i):
        xa, xb_, xc = xs[i], xs[i + 1], xs[i + 3]
        high, low = tile_hi[i], tile_lo[i]
        B = BLOCK
        acc[sweep, i] += (times(high[:, :B], low[:, :B], xa, 1)
                          + times(high[:, B : 2 * B], low[:, B : 2 * B], xb_, 1)
                          + times(high[:, 2 * B : 3 * B], low[:, 2 * B : 3 * B], xc, 1))
        down = times(high[:, B : 3 * B], low[:, B : 3 * B], xa, 0)
        acc[sweep, i + 1] += down[:B] + times(high[:, 3 * B :], low[:, 3 * B :], xc, 1)
        acc[sweep, i + 3] += down[B:] + times(high[:, 3 * B :], low[:, 3 * B :], xb_, 0)

    def take(step, i):
        pair[step].wait_recv()
        tile_hi[i], tile_lo[i] = split(tiles[i])
        apply(0, i)

    take(0, j)
    for copy in near_copies:
        copy.wait_recv()
    onward = tile_to(side + mem * (over - side), (k * GROUP + over + mem * (side - over), mem))
    pair[1] = tile_to(side, partner)
    pair[2] = tile_to(over, partner)
    take(1, side)
    take(2, over)
    onward.wait_recv()
    pair[3] = tile_to(far, partner)
    take(3, far)

    for copy in targets[0]:
        copy.wait_recv()
    targets[1].wait()
    def back(sweep, n):
        return move.to(acc.at[sweep, GROUP + n], ret_in.at[sweep, n], plane(1))

    backs = [back(0, n) for n in range(2)]
    aheads = []
    for n in range(GROUP):
        px[n] = xb[n] + 0.5 * (tb[n] - xb[n] - acc[0, n])
        if n < REACH_DEV:
            aheads.append(move.to(px.at[n], halo_in.at[n], plane(planes - 1)))
    backs.append(back(0, 2))

    def settle(n, now):
        xs[n, :, :cols], xs[n, :, cols:] = split(now)
        if n < GROUP:
            final[n] = now + 0.5 * (tb[n] - now)

    def settle_own(n):
        backs[n].wait_recv()
        settle(n, px[n] - 0.5 * ret_in[0, n])

    def settle_halo(n):
        aheads[n].wait_recv()
        settle(GROUP + n, halo_in[n] - 0.5 * acc[0, GROUP + n])

    place = pl.ds(pl.multiple_of(j * cols, cols), cols)
    base = move.sent
    here_sem = local_sem.at[move.local]

    def leave(n, source):
        return pltpu.make_async_remote_copy(
            src_ref=final.at[n], dst_ref=out.at[:, place],
            send_sem=send_sem.at[base + n], recv_sem=recv_sem.at[base + source],
            device_id=(k * GROUP + n, mem), device_id_type=pl.DeviceIdType.MESH,
        )

    def stay(n):
        return pltpu.make_async_copy(final.at[n], out.at[:, place], here_sem)

    def put(n):
        @pl.when(j != n)
        def _():
            leave(n, j).start()

        @pl.when(j == n)
        def _():
            stay(n).start()

    move.sent = base + GROUP
    settle(GROUP - 1, px[GROUP - 1])
    settle_own(0)
    settle_own(1)
    apply(1, 0)
    settle_own(2)
    settle_halo(0)
    apply(1, 1)
    settle_halo(1)
    apply(1, 2)
    backs = {1: back(1, 1)}
    settle_halo(2)
    apply(1, 3)
    backs[0] = back(1, 0)
    backs[2] = back(1, 2)
    final[3] = final[3] - 0.5 * acc[1, 3]
    put(3)
    for n in (1, 0, 2):
        backs[n].wait_recv()
        final[n] = final[n] - 0.5 * (acc[1, n] + ret_in[1, n])
        put(n)
    for n in range(GROUP):
        @pl.when(j != n)
        def _():
            leave(n, n).wait_send()
            leave(n, n).wait_recv()

        @pl.when(j == n)
        def _():
            stay(n).wait()
    for copy in move.open:
        copy.wait_send()


def in_one_kernel(perturb, pair_list, pair_count, band_weight, cov_scale, target, first_guess):
    w = gap_weights(pair_list, pair_count, band_weight, cov_scale)
    table = jnp.broadcast_to(jnp.pad(w, (0, 8 - w.shape[0]))[:, None], (8, BLOCK))
    planes = lax.axis_size("space") // GROUP
    rows = perturb.shape[0]
    cols = first_guess.shape[1] // GROUP
    f32, bf16 = jnp.float32, jnp.bfloat16
    sends = 2 * (planes - 1) + 1 + planes * 2 * (GROUP - 1) + 2 * (GROUP - 1) + 1 + 1
    sends += 3 + GROUP + 1 + 3 * REACH_DEV + GROUP
    locals_ = 2 + 2 * planes + 2 + 1
    vmem = pl.BlockSpec(memory_space=pltpu.VMEM)
    hbm = pl.BlockSpec(memory_space=pltpu.HBM)
    return pl.pallas_call(
        functools.partial(kernel, planes),
        out_shape=jax.ShapeDtypeStruct(first_guess.shape, f32),
        in_specs=[hbm, vmem, hbm, hbm],
        out_specs=vmem,
        scratch_shapes=[
            pltpu.VMEM((planes, rows, NEAR * BLOCK), f32),
            pltpu.VMEM((planes, GROUP, rows, 3 * BLOCK), f32),
            pltpu.VMEM((BLOCK, 4 * BLOCK), f32),
            pltpu.VMEM((BLOCK // 2, 4 * BLOCK), f32),
            pltpu.VMEM((8, BLOCK), f32),
            pltpu.VMEM((GROUP, BLOCK, 4 * BLOCK), f32),
            pltpu.VMEM((GROUP, BLOCK, 4 * BLOCK), bf16),
            pltpu.VMEM((GROUP, BLOCK, 4 * BLOCK), bf16),
            pltpu.VMEM((GROUP, BLOCK, cols), f32),
            pltpu.VMEM((GROUP, BLOCK, cols), f32),
            pltpu.VMEM((REACH_DEV, BLOCK, cols), f32),
            pltpu.VMEM((NEAR, BLOCK, 2 * cols), bf16),
            pltpu.VMEM((2, NEAR, BLOCK, cols), f32),
            pltpu.VMEM((GROUP, BLOCK, cols), f32),
            pltpu.VMEM((2, REACH_DEV, BLOCK, cols), f32),
            pltpu.VMEM((REACH_DEV, BLOCK, cols), f32),
            pltpu.VMEM((GROUP, BLOCK, cols), f32),
            pltpu.SemaphoreType.DMA((sends,)),
            pltpu.SemaphoreType.DMA((sends,)),
            pltpu.SemaphoreType.DMA((locals_,)),
        ],
        compiler_params=pltpu.CompilerParams(
            collective_id=0, has_side_effects=True, vmem_limit_bytes=48 * 1024 * 1024
        ),
    )(perturb, table, first_guess, target)


def fits(perturb, field):
    planes, rest = divmod(lax.axis_size("space"), GROUP)
    return (
        lax.axis_size("mem") == 2 and rest == 0 and planes >= 2
        and perturb.shape[0] % 8 == 0 and field.shape[1] % (GROUP * 128) == 0
        and field.shape[0] == BLOCK
    )


def per_device(perturb, pair_list, pair_count, band_weight, cov_scale, target, first_guess):
    whole = in_one_kernel if fits(perturb, first_guess) else by_collectives
    return whole(perturb, pair_list, pair_count, band_weight, cov_scale, target, first_guess)


def solution(mesh):
    in_specs = (
        P(("space", "mem"), None),
        P("space", None),
        P("space"),
        P(),
        P(),
        P("space", "mem"),
        P("space", "mem"),
    )
    out_specs = P("space", "mem")
    return jax.shard_map(
        per_device, mesh=mesh, in_specs=in_specs, out_specs=out_specs, check_vma=False
    )
```
